32 devices in a mesh: ctx: 8 (over z, y), chan: 4 (over x, core).
Axes of the slice: x: 2, y: 2, z: 4, core: 2. Of those that a mesh axis runs over, the one named last changes fastest.
Arguments:
- signal: bfloat16 [64, 65536], P('chan', 'ctx'), may hold values from -6 to 6
- filter_taps: bfloat16 [4, 65536], P('chan', 'ctx'), may hold values from -1 to 1
- gate_values: bfloat16 [64, 65536], P('chan', 'ctx'), may hold values from -6 to 6
- skip_weight: float32 [64], P('chan'), may hold values from -4 to 4
Outputs:
- gated_output: bfloat16 [64, 65536], P('chan', 'ctx')
The draws below stay inside these ranges and needn't reach their ends.
All inputs are finite; a program needn't handle non-finite values.
Results may differ from the reference program's by a relative error of at most 0.001.
Values may be sent and summed in bfloat16 or wider, within the bound.
No kernel may reach another device: no remote copies, remote signals or barrier semaphores. Data moves between devices by JAX's collectives and lax.ppermute only.
A program may use at most 64 MiB of HBM per device.

```python
import math
import jax
import jax.numpy as jnp
from jax import lax

GROUP = 16
SEQ = 65536
CHANNELS = 64
FILTERS = 4


def draw_filter_taps(key, part):
    positions = jnp.arange(SEQ, dtype=jnp.float32)[None, :]

    def add_mode(mode_index, accum):
        subkeys = jax.random.split(jax.random.fold_in(key, mode_index), 5)
        slow_rate = jnp.exp(jax.random.uniform(subkeys[0], (FILTERS, 1), jnp.float32, math.log(0.5 / SEQ), math.log(2.0 / SEQ)))
        fast_rate = jnp.exp(jax.random.uniform(subkeys[1], (FILTERS, 1), jnp.float32, math.log(1.0 / 2000.0), math.log(1.0 / 30.0)))
        is_slow = jax.random.uniform(subkeys[4], (FILTERS, 1), jnp.float32) < 0.5
        decay_rate = jnp.where(is_slow, slow_rate, fast_rate)
        frequency = jax.random.uniform(subkeys[2], (FILTERS, 1), jnp.float32, 0.0, math.pi)
        offset_angle = jax.random.uniform(subkeys[3], (FILTERS, 1), jnp.float32, -math.pi, math.pi)
        amplitude = jax.random.normal(jax.random.fold_in(subkeys[3], 7), (FILTERS, 1), jnp.float32)
        return accum + amplitude * jnp.exp(-decay_rate * positions) * jnp.cos(frequency * positions + offset_angle)
    modal_sum = lax.fori_loop(0, 16, add_mode, jnp.zeros((FILTERS, SEQ), jnp.float32))
    rough_factor = jax.random.uniform(jax.random.fold_in(key, 1000), (FILTERS, SEQ), jnp.float32, 0.5, 1.5)
    tap_values = modal_sum * rough_factor
    row_norm = jnp.sqrt(jnp.sum(tap_values * tap_values, axis=1, keepdims=True))
    return (tap_values / row_norm).astype(jnp.bfloat16)


def levels(key, shape, shards, least, high):
    def one(dim, parts):
        heights = jax.random.uniform(jax.random.fold_in(jax.random.fold_in(key, 6), dim), (parts,), jnp.float32, least / len(shards), high / len(shards))
        return jnp.repeat(jnp.exp(heights), shape[dim] // parts).reshape((-1,) + (1,) * (len(shape) - dim - 1))

    factor_of = one(*shards[0])
    for cut in shards[1:]:
        factor_of = factor_of * one(*cut)
    return factor_of


def normal_values(own_key, shape, deviation, most, cuts=(), held_as=jnp.bfloat16):
    loudness = levels(own_key, shape, cuts, -0.22, 0.18) if cuts else 1.0
    values = jax.random.normal(own_key, shape, jnp.float32) * deviation * loudness
    return jnp.minimum(jnp.maximum(values, -most), most).astype(held_as)


def setup_inputs(seed: int = 0) -> dict:
    key_of = jax.random.split(jax.random.key(seed), 5)
    signal = normal_values(key_of[0], (CHANNELS, SEQ), 1.0, 6.0, ((0, 4), (1, 8)))
    filter_taps = draw_filter_taps(jax.random.fold_in(key_of[4], 71), 0)
    gate_values = normal_values(key_of[2], (CHANNELS, SEQ), 1.0, 6.0, ((0, 4), (1, 8)))
    skip_weight = normal_values(key_of[3], (CHANNELS,), 1.0, 4.0, ((0, 4),), jnp.float32)
    return dict(signal=signal, filter_taps=filter_taps, gate_values=gate_values, skip_weight=skip_weight)


def reference(signal, filter_taps, gate_values, skip_weight):
    seq_length = signal.shape[1]

    def convolve_row(channel):
        signal_row = signal[channel].astype(jnp.float32)
        tap_row = filter_taps[channel // GROUP].astype(jnp.float32)
        spectrum = jnp.fft.fft(jnp.pad(signal_row, (0, seq_length)))
        taps_spectrum = jnp.fft.fft(jnp.pad(tap_row, (0, seq_length)))
        return jnp.real(jnp.fft.ifft(spectrum * taps_spectrum))[:seq_length]

    convolved = lax.map(convolve_row, jnp.arange(CHANNELS, dtype=jnp.int32))
    mixed = gate_values.astype(jnp.float32) * (convolved + skip_weight[:, None] * signal.astype(jnp.float32))
    return mixed.astype(jnp.bfloat16)
```

```python
import functools
import math

import jax
import jax.numpy as jnp
import numpy as np
from jax import lax
from jax.experimental import pallas as pl
from jax.experimental.pallas import tpu as pltpu
from jax.sharding import PartitionSpec as P

BF16 = jnp.bfloat16
F32 = jnp.float32


def two_parts(table):
    high = table.astype(BF16)
    low = (table - high.astype(np.float64)).astype(BF16)
    return np.stack([high, low])


def tables_of(rows, cols):
    total = rows * cols
    row = np.arange(rows, dtype=np.float64)
    col = np.arange(cols, dtype=np.float64)
    head = 2.0 * np.pi * ((4 * row[:, None] + 1) * row[None, :] % (4 * rows)) / (4 * rows)
    turn = 2.0 * np.pi * ((4 * row[:, None] + 1) * col[None, :]) / (4 * total)
    tail = 2.0 * np.pi * (col[:, None] * col[None, :] % cols) / cols
    first = two_parts(np.concatenate([np.cos(head), np.sin(head)], 0))
    twist = np.stack([np.cos(turn), np.sin(turn)]).astype(np.float32)
    middle = two_parts(np.concatenate([np.cos(tail), np.sin(tail)], 0))
    last = two_parts(np.concatenate([np.cos(head).T, np.sin(head).T], 1) / total)
    return first, twist, middle, last


def matmul(left, right):
    return jnp.dot(left, right, preferred_element_type=F32)


def split(value):
    high = value.astype(BF16)
    return high, (value - high.astype(F32)).astype(BF16)


LANES = 128


def pack_kernel(signal_ref, taps_ref, out_ref, work_ref):
    channels, length = signal_ref.shape
    shards, rows, lines, width = out_ref.shape
    each = rows - 1
    for line in range(lines):
        for part in range(width // LANES):
            start = line * width + part * LANES
            work_ref[part, pl.ds(line, channels, stride=lines), :] = signal_ref[
                :, start : start + LANES
            ].astype(F32)
    for part in range(width // LANES):
        span = slice(part * LANES, (part + 1) * LANES)
        for shard in range(shards):
            for row in range(each):
                start = (shard * each + row) * lines
                out_ref[shard, row, :, span] = work_ref[part, start : start + lines, :].astype(BF16)
    for line in range(lines):
        for part in range(width // LANES):
            start = line * width + part * LANES
            work_ref[part, line : line + 1, :] = taps_ref[:, start : start + LANES].astype(F32)
    for part in range(width // LANES):
        span = slice(part * LANES, (part + 1) * LANES)
        taps = work_ref[part, 0:lines, :].astype(BF16)
        for shard in range(shards):
            out_ref[shard, each, :, span] = taps


def conv_kernel(
    data_ref, first_ref, twist_ref, middle_ref, last_ref, out_ref, high_ref, low_ref, spec_ref, col_ref
):
    shards, rows, lines, width = data_ref.shape
    each = rows - 1
    size = shards * lines

    def forward(row):
        data = data_ref[:, row].reshape(size, width)
        part = matmul(first_ref[0], data) + matmul(first_ref[1], data)
        real, imag = part[:size], part[size:]
        cosine, sine = twist_ref[0], twist_ref[1]
        real, imag = real * cosine - imag * sine, real * sine + imag * cosine
        for ref, pair in zip((high_ref, low_ref), zip(split(real), split(imag))):
            ref[:size, :width] = pair[0]
            ref[:size, width:] = -pair[1]
            ref[size:, :width] = pair[1]
            ref[size:, width:] = pair[0]
        return mixed()

    def mixed():
        return (
            matmul(high_ref[...], middle_ref[0])
            + matmul(low_ref[...], middle_ref[0])
            + matmul(high_ref[...], middle_ref[1])
        )

    spec_ref[...] = forward(each)
    for row in range(each):
        part = forward(row)
        real, imag = part[:size], part[size:]
        other_real, other_imag = spec_ref[:size], spec_ref[size:]
        real, imag = real * other_real - imag * other_imag, real * other_imag + imag * other_real
        for ref, pair in zip((high_ref, low_ref), zip(split(real), split(imag))):
            ref[:size, :width] = pair[0]
            ref[:size, width:] = pair[1]
            ref[size:, :width] = pair[1]
            ref[size:, width:] = -pair[0]
        part = mixed()
        real, imag = part[:size], part[size:]
        cosine, sine = twist_ref[0], twist_ref[1]
        real, imag = real * cosine + imag * sine, imag * cosine - real * sine
        for index, pair in enumerate(zip(split(real), split(imag))):
            col_ref[index, :size] = pair[0]
            col_ref[index, size:] = pair[1]
        result = (
            matmul(last_ref[0], col_ref[0])
            + matmul(last_ref[0], col_ref[1])
            + matmul(last_ref[1], col_ref[0])
        )
        out_ref[:, row] = result.reshape(shards, lines, width)


def finish_kernel(conv_ref, signal_ref, gate_ref, skip_ref, out_ref, work_ref):
    channels, length = signal_ref.shape
    total, width = conv_ref.shape
    lines = length // width
    for part in range(width // LANES):
        work_ref[part] = conv_ref[:, part * LANES : (part + 1) * LANES]
    for line in range(lines):
        for part in range(width // LANES):
            start = line * width + part * LANES
            span = slice(start, start + LANES)
            conv = work_ref[part, pl.ds(line, channels, stride=lines), :]
            mixed = gate_ref[:, span].astype(F32) * (
                conv + skip_ref[...] * signal_ref[:, span].astype(F32)
            )
            out_ref[:, span] = mixed.astype(BF16)


def local(signal, filter_taps, gate_values, skip_weight):
    channels, length = signal.shape
    shards = lax.axis_size("ctx")
    total = shards * length
    width = 1 << ((total.bit_length() - 1) // 2)
    lines = length // width
    size = shards * lines
    each = -(-channels // shards)
    spare = each * shards - channels
    padded = jnp.pad(signal, ((0, spare), (0, 0))) if spare else signal
    packed = pl.pallas_call(
        pack_kernel,
        out_shape=jax.ShapeDtypeStruct((shards, each + 1, lines, width), BF16),
        scratch_shapes=[pltpu.VMEM((width // LANES, each * shards * lines, LANES), F32)],
    )(padded, filter_taps)
    data = lax.all_to_all(packed, "ctx", split_axis=0, concat_axis=0, tiled=True)
    first, twist, middle, last = (jnp.asarray(table) for table in tables_of(size, width))
    convolved = pl.pallas_call(
        conv_kernel,
        out_shape=jax.ShapeDtypeStruct((shards, each, lines, width), F32),
        scratch_shapes=[
            pltpu.VMEM((2 * size, 2 * width), BF16),
            pltpu.VMEM((2 * size, 2 * width), BF16),
            pltpu.VMEM((2 * size, width), F32),
            pltpu.VMEM((2, 2 * size, width), BF16),
        ],
    )(data, first, twist, middle, last)
    own = lax.all_to_all(convolved, "ctx", split_axis=0, concat_axis=0, tiled=True)
    own = own.reshape(each * shards * lines, width)
    return pl.pallas_call(
        finish_kernel,
        out_shape=jax.ShapeDtypeStruct((channels, length), BF16),
        scratch_shapes=[pltpu.VMEM((width // LANES, each * shards * lines, LANES), F32)],
    )(own, signal, gate_values, skip_weight[:, None])


def solution(mesh):
    return jax.shard_map(
        local,
        mesh=mesh,
        in_specs=(P("chan", "ctx"), P("chan", "ctx"), P("chan", "ctx"), P("chan")),
        out_specs=P("chan", "ctx"),
        check_vma=False,
    )
```

```python
import functools
import math

import jax
import jax.numpy as jnp
import numpy as np
from jax import lax
from jax.experimental import pallas as pl
from jax.experimental.pallas import tpu as pltpu
from jax.sharding import PartitionSpec as P

BF16 = jnp.bfloat16
F32 = jnp.float32


def two_parts(table):
    high = table.astype(BF16)
    low = (table - high.astype(np.float64)).astype(BF16)
    return np.stack([high, low])


def tables_of(rows, cols):
    total = rows * cols
    row = np.arange(rows, dtype=np.float64)
    col = np.arange(cols, dtype=np.float64)
    head = 2.0 * np.pi * ((4 * row[:, None] + 1) * row[None, :] % (4 * rows)) / (4 * rows)
    turn = 2.0 * np.pi * ((4 * row[:, None] + 1) * col[None, :]) / (4 * total)
    tail = 2.0 * np.pi * (col[:, None] * col[None, :] % cols) / cols
    first = two_parts(np.concatenate([np.cos(head), np.sin(head)], 0))
    twist = np.stack([np.cos(turn), np.sin(turn)]).astype(np.float32)
    middle = two_parts(np.concatenate([np.cos(tail), np.sin(tail)], 0))
    last = two_parts(np.concatenate([np.cos(head).T, np.sin(head).T], 1) / total)
    return first, twist, middle, last


def matmul(left, right):
    return jnp.dot(left, right, preferred_element_type=F32)


def split(value):
    high = value.astype(BF16)
    return high, (value - high.astype(F32)).astype(BF16)


LANES = 128


def partner(position, step, shards):
    if shards & (shards - 1) == 0:
        return position ^ step
    return (2 * shards + step - position) % shards


def spread(source_ref, work_ref, lines):
    channels, length = source_ref.shape
    width = length // lines
    for line in range(lines):
        for part in range(width // LANES):
            start = line * width + part * LANES
            work_ref[part, pl.ds(line, channels, stride=lines), :] = source_ref[
                :, start : start + LANES
            ].astype(F32)


def pack_kernel(source_ref, taps_ref, out_ref, work_ref):
    shards, rows, lines, width = out_ref.shape
    each = rows - 1
    spread(source_ref, work_ref, lines)
    for part in range(width // LANES):
        span = slice(part * LANES, (part + 1) * LANES)
        for shard in range(shards):
            for row in range(each):
                start = (shard * each + row) * lines
                out_ref[shard, row, :, span] = work_ref[part, start : start + lines, :].astype(BF16)
    spread(taps_ref, work_ref, lines)
    for part in range(width // LANES):
        span = slice(part * LANES, (part + 1) * LANES)
        taps = work_ref[part, 0:lines, :].astype(BF16)
        for shard in range(shards):
            out_ref[shard, each, :, span] = taps


def gate_pack_kernel(source_ref, *refs):
    out_refs, work_ref = refs[:-1], refs[-1]
    each, lines, width = out_refs[0].shape
    shards = len(out_refs)
    spread(source_ref, work_ref, lines)
    position = lax.axis_index("ctx")
    for step, out_ref in enumerate(out_refs):
        target = partner(position, step, shards)
        for part in range(width // LANES):
            span = slice(part * LANES, (part + 1) * LANES)
            for row in range(each):
                start = pl.multiple_of((target * each + row) * lines, lines)
                out_ref[row, :, span] = work_ref[part, pl.ds(start, lines), :].astype(BF16)


def conv_kernel(
    data_ref, skip_ref, first_ref, twist_ref, middle_ref, last_ref, out_ref, high_ref, low_ref, spec_ref, col_ref
):
    shards, rows, lines, width = data_ref.shape
    each = rows - 1
    size = shards * lines

    def forward(row):
        data = data_ref[:, row].reshape(size, width)
        part = matmul(first_ref[0], data) + matmul(first_ref[1], data)
        real, imag = part[:size], part[size:]
        cosine, sine = twist_ref[0], twist_ref[1]
        real, imag = real * cosine - imag * sine, real * sine + imag * cosine
        for ref, pair in zip((high_ref, low_ref), zip(split(real), split(imag))):
            ref[:size, :width] = pair[0]
            ref[:size, width:] = -pair[1]
            ref[size:, :width] = pair[1]
            ref[size:, width:] = pair[0]
        return mixed()

    def mixed():
        return (
            matmul(high_ref[...], middle_ref[0])
            + matmul(low_ref[...], middle_ref[0])
            + matmul(high_ref[...], middle_ref[1])
        )

    spec_ref[...] = forward(each)
    for row in range(each):
        part = forward(row)
        real, imag = part[:size], part[size:]
        other_real, other_imag = spec_ref[:size], spec_ref[size:]
        real, imag = real * other_real - imag * other_imag, real * other_imag + imag * other_real
        for ref, pair in zip((high_ref, low_ref), zip(split(real), split(imag))):
            ref[:size, :width] = pair[0]
            ref[:size, width:] = pair[1]
            ref[size:, :width] = pair[1]
            ref[size:, width:] = -pair[0]
        part = mixed()
        real, imag = part[:size], part[size:]
        cosine, sine = twist_ref[0], twist_ref[1]
        real, imag = real * cosine + imag * sine, imag * cosine - real * sine
        for index, pair in enumerate(zip(split(real), split(imag))):
            col_ref[index, :size] = pair[0]
            col_ref[index, size:] = pair[1]
        result = (
            matmul(last_ref[0], col_ref[0])
            + matmul(last_ref[0], col_ref[1])
            + matmul(last_ref[1], col_ref[0])
        )
        weight = skip_ref[lax.axis_index("ctx") * each + row]
        out_ref[:, row] = result.reshape(shards, lines, width) + weight * data_ref[:, row].astype(F32)


def gate_kernel(conv_ref, *refs):
    gate_refs, out_ref = refs[:-1], refs[-1]
    shards, each, lines, width = conv_ref.shape
    position = lax.axis_index("ctx")
    for step, gate_ref in enumerate(gate_refs):
        shard = partner(position, step, shards)
        for row in range(each):
            mixed = gate_ref[row].astype(F32) * conv_ref[shard, row]
            out_ref[shard, row] = mixed.astype(BF16)


def unpack_kernel(source_ref, out_ref, work_ref):
    channels, length = out_ref.shape
    shards, each, lines, width = source_ref.shape
    for part in range(width // LANES):
        span = slice(part * LANES, (part + 1) * LANES)
        for shard in range(shards):
            for row in range(each):
                start = (shard * each + row) * lines
                work_ref[part, start : start + lines, :] = source_ref[shard, row, :, span].astype(F32)
    for line in range(lines):
        for part in range(width // LANES):
            start = line * width + part * LANES
            out_ref[:, start : start + LANES] = work_ref[
                part, pl.ds(line, channels, stride=lines), :
            ].astype(BF16)


def kernel_call(body, out_shape, scratch=(), limit=12):
    return pl.pallas_call(
        body,
        out_shape=out_shape,
        scratch_shapes=list(scratch),
        compiler_params=pltpu.CompilerParams(vmem_limit_bytes=limit * 2**20),
    )


def local(signal, filter_taps, gate_values, skip_weight):
    channels, length = signal.shape
    shards = lax.axis_size("ctx")
    total = shards * length
    width = 1 << ((total.bit_length() - 1) // 2)
    lines = length // width
    size = shards * lines
    each = -(-channels // shards)
    spare = each * shards - channels
    skip = skip_weight
    gate = gate_values
    padded = signal
    if spare:
        padded = jnp.pad(signal, ((0, spare), (0, 0)))
        gate = jnp.pad(gate, ((0, spare), (0, 0)))
        skip = jnp.pad(skip, (0, spare))
    work = pltpu.VMEM((width // LANES, each * shards * lines, LANES), F32)
    block = (shards, each, lines, width)
    packed = kernel_call(
        pack_kernel, jax.ShapeDtypeStruct((shards, each + 1, lines, width), BF16), [work], 60
    )(padded, filter_taps)
    data = lax.all_to_all(packed, "ctx", split_axis=0, concat_axis=0, tiled=True)
    gates = kernel_call(
        gate_pack_kernel, [jax.ShapeDtypeStruct(block[1:], BF16)] * shards, [work]
    )(gate)
    gates = [gates[0]] + [
        lax.ppermute(gates[step], "ctx", [(j, partner(j, step, shards)) for j in range(shards)])
        for step in range(1, shards)
    ]
    first, twist, middle, last = (jnp.asarray(table) for table in tables_of(size, width))
    vmem = pl.BlockSpec(memory_space=pltpu.VMEM)
    convolved = pl.pallas_call(
        conv_kernel,
        out_shape=jax.ShapeDtypeStruct(block, F32),
        in_specs=[vmem, pl.BlockSpec(memory_space=pltpu.SMEM)] + [vmem] * 4,
        scratch_shapes=[
            pltpu.VMEM((2 * size, 2 * width), BF16),
            pltpu.VMEM((2 * size, 2 * width), BF16),
            pltpu.VMEM((2 * size, width), F32),
            pltpu.VMEM((2, 2 * size, width), BF16),
        ],
        compiler_params=pltpu.CompilerParams(vmem_limit_bytes=20 * 2**20),
    )(data, skip, first, twist, middle, last)
    mixed = pl.pallas_call(
        gate_kernel,
        out_shape=jax.ShapeDtypeStruct(block, BF16),
        compiler_params=pltpu.CompilerParams(vmem_limit_bytes=12 * 2**20),
    )(convolved, *gates)
    own = lax.all_to_all(mixed, "ctx", split_axis=0, concat_axis=0, tiled=True)
    result = kernel_call(
        unpack_kernel, jax.ShapeDtypeStruct((each * shards, length), BF16), [work]
    )(own)
    return result[:channels]


def solution(mesh):
    return jax.shard_map(
        local,
        mesh=mesh,
        in_specs=(P("chan", "ctx"), P("chan", "ctx"), P("chan", "ctx"), P("chan")),
        out_specs=P("chan", "ctx"),
        check_vma=False,
    )
```

```python
import functools
import math

import jax
import jax.numpy as jnp
import numpy as np
from jax import lax
from jax.experimental import pallas as pl
from jax.experimental.pallas import tpu as pltpu
from jax.sharding import PartitionSpec as P

BF16 = jnp.bfloat16
F32 = jnp.float32


def two_parts(table):
    high = table.astype(BF16)
    low = (table - high.astype(np.float64)).astype(BF16)
    return np.stack([high, low])


def tables_of(rows, cols):
    total = rows * cols
    row = np.arange(rows, dtype=np.float64)
    col = np.arange(cols, dtype=np.float64)
    head = 2.0 * np.pi * ((4 * row[:, None] + 1) * row[None, :] % (4 * rows)) / (4 * rows)
    turn = 2.0 * np.pi * ((4 * row[:, None] + 1) * col[None, :]) / (4 * total)
    tail = 2.0 * np.pi * (col[:, None] * col[None, :] % cols) / cols
    twist = two_parts(np.concatenate([np.cos(turn), np.sin(turn)], 0))
    first = two_parts(np.concatenate([np.cos(head), np.sin(head)], 0))
    middle = two_parts(np.concatenate([np.cos(tail), np.sin(tail)], 0))
    last = two_parts(np.concatenate([np.cos(head).T, np.sin(head).T], 0) / total)
    if rows == cols:
        return (np.stack([twist, first, middle, last]),)
    return twist, first, middle, last


def matmul(left, right):
    return jnp.dot(left, right, preferred_element_type=F32)


def split(value):
    high = value.astype(BF16)
    return high, (value - high.astype(F32)).astype(BF16)


LANES = 128


def spread(source_ref, work_ref, lines, first=0, count=None):
    channels, length = source_ref.shape
    width = length // lines
    for line in range(first, lines if count is None else first + count):
        for part in range(width // LANES):
            start = line * width + part * LANES
            work_ref[part, pl.ds(line, channels, stride=lines), :] = source_ref[
                :, start : start + LANES
            ].astype(F32)


def partner(position, step, shards):
    if shards & (shards - 1) == 0:
        return position ^ step
    return (2 * shards + step - position) % shards


def pack_kernel(*refs):
    source_hbm, taps_hbm, gate_hbm, skip_hbm, out_hbm, weight_ref = refs[:6]
    gates, scratch = refs[6:-10], refs[-10:]
    source_ref, taps_ref, gate_ref, skip_ref, work_ref, tail_ref, out_ref = scratch[:7]
    in_sems, out_sems, rest_sems = scratch[7:]
    channels, length = source_hbm.shape
    shards, rows, lines, width = out_hbm.shape
    each = rows - 1
    chunks = out_sems.shape[0]
    count = lines // chunks
    reads = []
    for chunk in range(chunks):
        span = pl.ds(chunk * count * width, count * width)
        reads.append(
            pltpu.make_async_copy(
                source_hbm.at[:, span], source_ref.at[:, span], in_sems.at[chunk]
            )
        )
    reads.append(pltpu.make_async_copy(taps_hbm, taps_ref, in_sems.at[chunks]))
    rest = [
        pltpu.make_async_copy(gate_hbm, gate_ref, rest_sems.at[0]),
        pltpu.make_async_copy(skip_hbm, skip_ref, rest_sems.at[1]),
    ]
    for read in reads + rest:
        read.start()
    writes = []
    for chunk in range(chunks):
        first = chunk * count
        reads[chunk].wait()
        spread(source_ref, work_ref, lines, first, count)
        if chunk == 0:
            reads[chunks].wait()
        spread(taps_ref, tail_ref, lines, first, count)
        for part in range(width // LANES):
            span = slice(part * LANES, (part + 1) * LANES)
            taps = tail_ref[part, first : first + count, :].astype(BF16)
            for shard in range(shards):
                for row in range(each):
                    start = (shard * each + row) * lines + first
                    out_ref[shard, row, first : first + count, span] = work_ref[
                        part, start : start + count, :
                    ].astype(BF16)
                out_ref[shard, each, first : first + count, span] = taps
        span = pl.ds(first, count)
        write = pltpu.make_async_copy(
            out_ref.at[:, :, span, :], out_hbm.at[:, :, span, :], out_sems.at[chunk]
        )
        write.start()
        writes.append(write)
    for copy in rest:
        copy.wait()
    position = lax.axis_index("ctx")
    for row in range(each):
        weight_ref[row] = jnp.full(weight_ref.shape[1:], skip_ref[position * each + row], F32)
    spread(gate_ref, work_ref, lines)
    for step, block_ref in enumerate(gates):
        target = partner(position, step, shards)
        for part in range(width // LANES):
            span = slice(part * LANES, (part + 1) * LANES)
            for row in range(each):
                start = pl.multiple_of((target * each + row) * lines, lines)
                block_ref[row, :, span] = work_ref[part, pl.ds(start, lines), :].astype(BF16)
    for write in writes:
        write.wait()


def load_kernel(*refs):
    count = (len(refs) - 3) // 2
    tables_hbm, blocks = refs[0], refs[1 : 1 + count]
    tables_ref, outs, sem = refs[1 + count], refs[2 + count : -1], refs[-1]
    copy = pltpu.make_async_copy(tables_hbm, tables_ref, sem)
    copy.start()
    for source_ref, out_ref in zip(blocks, outs):
        out_ref[...] = source_ref[...]
    copy.wait()


def conv_kernel(
    data_ref, weight_ref, *refs
):
    *tables, out_ref, high_ref, low_ref, col_ref = refs
    if len(tables) == 1:
        tables = [tables[0].at[index] for index in range(4)]
    twist_ref, first_ref, middle_ref, last_ref = tables
    shards, rows, lines, width = data_ref.shape
    each = rows - 1
    size = shards * lines
    twist = twist_ref[0].astype(F32) + twist_ref[1].astype(F32)
    cosine, sine = twist[:size], twist[size:]

    def mixed(row):
        return (
            matmul(high_ref[row], middle_ref[0])
            + matmul(low_ref[row], middle_ref[0])
            + matmul(high_ref[row], middle_ref[1])
        )

    def forward(row):
        data = data_ref[:, row].reshape(size, width)
        part = matmul(first_ref[0], data) + matmul(first_ref[1], data)
        real, imag = part[:size], part[size:]
        real, imag = real * cosine - imag * sine, real * sine + imag * cosine
        for ref, pair in zip((high_ref, low_ref), zip(split(real), split(imag))):
            ref[row, :size, :width] = pair[0]
            ref[row, :size, width:] = -pair[1]
            ref[row, size:, :width] = pair[1]
            ref[row, size:, width:] = pair[0]

    for row in range(rows):
        forward(each - row)
    other = mixed(each)
    other_real, other_imag = other[:size], other[size:]
    for row in range(each):
        part = mixed(row)
        real, imag = part[:size], part[size:]
        real, imag = real * other_real - imag * other_imag, real * other_imag + imag * other_real
        for ref, pair in zip((high_ref, low_ref), zip(split(real), split(imag))):
            ref[rows + row, :size, :width] = pair[0]
            ref[rows + row, :size, width:] = pair[1]
            ref[rows + row, size:, :width] = pair[1]
            ref[rows + row, size:, width:] = -pair[0]
    for row in range(each):
        part = mixed(rows + row)
        real, imag = part[:size], part[size:]
        real, imag = real * cosine + imag * sine, imag * cosine - real * sine
        for index, pair in enumerate(zip(split(real), split(imag))):
            col_ref[row, index, :size] = pair[0]
            col_ref[row, index, size:] = pair[1]
    for row in range(each):
        result = 0.0
        for part in range(2):
            span = slice(part * size, (part + 1) * size)
            result += (
                matmul(last_ref[0, span], col_ref[row, 0, span])
                + matmul(last_ref[0, span], col_ref[row, 1, span])
                + matmul(last_ref[1, span], col_ref[row, 0, span])
            )
        weight = weight_ref[row, :1, :1]
        out_ref[:, row] = result.reshape(shards, lines, width) + weight * data_ref[:, row].astype(F32)


TILE = 256
CHUNK = 32


def direct_conv_kernel(*refs):
    kinds = [pltpu.ACC(unit)((CHUNK, TILE), F32) for unit in range(2) for _ in range(3 * TILE // CHUNK)]
    pl.run_scoped(functools.partial(direct_conv_body, *refs), *kinds)


def direct_conv_body(
    data_ref,
    weight_ref,
    tables_ref,
    out_ref,
    high_ref,
    low_ref,
    turn_ref,
    spec_ref,
    col_ref,
    *accs,
):
    shards, rows, lines, width = data_ref.shape
    each = rows - 1
    count = TILE // CHUNK
    half = count // 2
    accs = [accs[: 3 * count], accs[3 * count :]]
    twist_ref, first_ref, middle_ref, last_ref = (tables_ref.at[index] for index in range(4))
    units = range(2)
    channels = [list(range(unit, each, 2)) for unit in units]

    def push(unit, value, slot):
        pltpu.matmul_push_rhs(value, slot, unit)

    def add(unit, index, value, slot=None):
        pltpu.matmul_acc_lhs(accs[unit][index], value, slot)

    def pop(unit, index):
        return pltpu.matmul_pop(accs[unit][index])

    def chunk_of(index):
        return slice(index * CHUNK, (index + 1) * CHUNK)

    def store(row, index, real, imag, signs):
        for ref, (one, two) in zip((high_ref, low_ref), zip(split(real), split(imag))):
            ref[row, 0, chunk_of(index)] = one
            ref[row, 1, chunk_of(index)] = two
            ref[row, 2, chunk_of(index)] = -two if signs else -one

    def products(unit, slots, row_parts):
        for step, (part, tile) in enumerate(((0, 0), (0, 1), (1, 0), (1, 1))):
            slot = step % 2
            push(unit, middle_ref[part, tile * TILE : (tile + 1) * TILE], slot)
            load = slot
            for acc, operands, row, index in row_parts:
                refs = (high_ref, low_ref) if part == 0 else (high_ref,)
                for ref in refs:
                    add(unit, acc, ref[row, operands[tile], chunk_of(index)], load)
                    load = None

    for unit in units:
        push(unit, data_ref[:, each].reshape(TILE, TILE), 0)
    for unit in units:
        for index in range(count):
            span = slice(unit * TILE + index * CHUNK, unit * TILE + (index + 1) * CHUNK)
            add(unit, 2 * count + index, first_ref[0, span], 0 if index == 0 else None)
            add(unit, 2 * count + index, first_ref[1, span])
    for unit in units:
        for channel in channels[unit]:
            push(unit, data_ref[:, channel].reshape(TILE, TILE), 1)
            for index in range(count):
                for imag in range(2):
                    start = imag * TILE + index * CHUNK
                    span = slice(start, start + CHUNK)
                    load = 1 if index + imag == 0 else None
                    add(unit, 2 * index + imag, first_ref[0, span], load)
                    add(unit, 2 * index + imag, first_ref[1, span])

    for index in range(2 * count):
        span = chunk_of(index)
        turn_ref[span] = twist_ref[0, span].astype(F32) + twist_ref[1, span].astype(F32)

    def turn_of(index):
        return turn_ref[chunk_of(index)], turn_ref[chunk_of(count + index)]

    def turned(real, imag, index):
        cosine, sine = turn_of(index)
        return real * cosine - imag * sine, real * sine + imag * cosine

    for index in range(count):
        real, imag = pop(0, 2 * count + index), pop(1, 2 * count + index)
        store(each, index, *turned(real, imag, index), True)
    for unit in units:
        operands = (0, 2) if unit == 0 else (1, 0)
        products(unit, 0, [(2 * count + index, operands, each, index) for index in range(count)])
    for index in range(count):
        for unit in units:
            for channel in channels[unit]:
                real, imag = pop(unit, 2 * index), pop(unit, 2 * index + 1)
                store(channel, index, *turned(real, imag, index), True)
    for part in range(2):
        for unit in units:
            for channel in channels[unit]:
                products(
                    unit,
                    0,
                    [
                        (2 * index + imag, (1, 0) if imag else (0, 2), channel, index)
                        for index in range(part * half, (part + 1) * half)
                        for imag in range(2)
                    ],
                )
        if part == 0:
            for index in range(count):
                for unit in units:
                    spec_ref[unit, chunk_of(index)] = pop(unit, 2 * count + index)
    for part in range(2):
        for index in range(part * half, (part + 1) * half):
            other_real, other_imag = spec_ref[0, chunk_of(index)], spec_ref[1, chunk_of(index)]
            for unit in units:
                for channel in channels[unit]:
                    real, imag = pop(unit, 2 * index), pop(unit, 2 * index + 1)
                    store(
                        channel,
                        index,
                        real * other_real - imag * other_imag,
                        real * other_imag + imag * other_real,
                        False,
                    )
        for unit in units:
            for channel in channels[unit]:
                products(
                    unit,
                    0,
                    [
                        (2 * index + imag, (1, 2) if imag else (0, 1), channel, index)
                        for index in range(part * half, (part + 1) * half)
                        for imag in range(2)
                    ],
                )
    for index in range(count):
        cosine, sine = turn_of(index)
        for unit in units:
            for channel in channels[unit]:
                real, imag = pop(unit, 2 * index), pop(unit, 2 * index + 1)
                real, imag = real * cosine + imag * sine, imag * cosine - real * sine
                for place, pair in enumerate((split(real), split(imag))):
                    for part in range(2):
                        col_ref[channel, part, place, chunk_of(index)] = pair[part]
    for unit in units:
        for channel in channels[unit]:
            for step, (place, part) in enumerate(((0, 0), (1, 0), (0, 1), (1, 1))):
                slot = step % 2
                push(unit, col_ref[channel, part, place], slot)
                load = slot
                for index in range(count):
                    span = slice(place * TILE + index * CHUNK, place * TILE + (index + 1) * CHUNK)
                    for table in range(2 if part == 0 else 1):
                        add(unit, index, last_ref[table, span], load)
                        load = None
    per = lines // CHUNK
    for index in range(count):
        for unit in units:
            for channel in channels[unit]:
                result = pop(unit, index)
                weight = weight_ref[channel, :1]
                weight = jnp.concatenate([weight] * (width // LANES), 1)
                for shard in range(index // per, index // per + 1):
                    span = chunk_of(index % per)
                    out_ref[shard, channel, span] = result + weight * data_ref[
                        shard, channel, span
                    ].astype(F32)


def gate_kernel(conv_ref, *refs):
    gate_refs, out_ref = refs[:-1], refs[-1]
    shards, each, lines, width = conv_ref.shape
    position = lax.axis_index("ctx")
    for step, gate_ref in enumerate(gate_refs):
        shard = partner(position, step, shards)
        for row in range(each):
            out_ref[shard, row] = (gate_ref[row].astype(F32) * conv_ref[shard, row]).astype(BF16)


def unpack_kernel(source_ref, out_ref, work_ref):
    channels, length = out_ref.shape
    shards, each, lines, width = source_ref.shape
    for part in range(width // LANES):
        span = slice(part * LANES, (part + 1) * LANES)
        for shard in range(shards):
            for row in range(each):
                start = (shard * each + row) * lines
                work_ref[part, start : start + lines, :] = source_ref[shard, row, :, span].astype(F32)
    for line in range(lines):
        for part in range(width // LANES):
            start = line * width + part * LANES
            out_ref[:, start : start + LANES] = work_ref[
                part, pl.ds(line, channels, stride=lines), :
            ].astype(BF16)


def in_hbm(value):
    return pltpu.with_memory_space_constraint(value, pltpu.HBM)


def kernel_call(body, out_shape, scratch=(), limit=12):
    return pl.pallas_call(
        body,
        out_shape=out_shape,
        scratch_shapes=list(scratch),
        compiler_params=pltpu.CompilerParams(vmem_limit_bytes=limit * 2**20),
    )


def local(signal, filter_taps, gate_values, skip_weight):
    channels, length = signal.shape
    shards = lax.axis_size("ctx")
    total = shards * length
    width = 1 << ((total.bit_length() - 1) // 2)
    lines = length // width
    size = shards * lines
    each = -(-channels // shards)
    spare = each * shards - channels
    skip = skip_weight
    gate = gate_values
    padded = signal
    if spare:
        padded = jnp.pad(signal, ((0, spare), (0, 0)))
        gate = jnp.pad(gate, ((0, spare), (0, 0)))
        skip = jnp.pad(skip, (0, spare))
    work = pltpu.VMEM((width // LANES, each * shards * lines, LANES), F32)
    block = (shards, each, lines, width)
    hbm = pl.BlockSpec(memory_space=pltpu.HBM)
    vmem = pl.BlockSpec(memory_space=pltpu.VMEM)
    chunks = max(1, lines // 16)
    packed, weights, *gates = pl.pallas_call(
        pack_kernel,
        out_shape=[
            jax.ShapeDtypeStruct((shards, each + 1, lines, width), BF16),
            jax.ShapeDtypeStruct((each, 8, LANES), F32),
        ]
        + [jax.ShapeDtypeStruct(block[1:], BF16)] * shards,
        in_specs=[hbm] * 4,
        out_specs=[hbm] + [vmem] * (shards + 1),
        scratch_shapes=[
            pltpu.VMEM((each * shards, length), BF16),
            pltpu.VMEM((1, length), BF16),
            pltpu.VMEM((each * shards, length), BF16),
            pltpu.SMEM((each * shards,), F32),
            work,
            pltpu.VMEM((width // LANES, lines, LANES), F32),
            pltpu.VMEM((shards, each + 1, lines, width), BF16),
            pltpu.SemaphoreType.DMA((chunks + 1,)),
            pltpu.SemaphoreType.DMA((chunks,)),
            pltpu.SemaphoreType.DMA((2,)),
        ],
        compiler_params=pltpu.CompilerParams(vmem_limit_bytes=12 * 2**20),
    )(*(in_hbm(value) for value in (padded, filter_taps, gate, skip)))
    with jax.named_scope("first_swap"):
        data = lax.all_to_all(packed, "ctx", split_axis=0, concat_axis=0, tiled=True)
    tables = tuple(jnp.asarray(table) for table in tables_of(size, width))
    near = shards // 2
    if len(tables) == 1 and shards > 1:
        tables, *gates[near:] = pl.pallas_call(
            load_kernel,
            out_shape=[
                jax.ShapeDtypeStruct(value.shape, BF16) for value in (*tables, *gates[near:])
            ],
            in_specs=[hbm] + [vmem] * (shards - near),
            out_specs=[vmem] * (1 + shards - near),
            scratch_shapes=[pltpu.SemaphoreType.DMA],
            compiler_params=pltpu.CompilerParams(vmem_limit_bytes=8 * 2**20),
        )(in_hbm(tables[0]), *gates[near:])
        tables = (tables,)
    for step in range(1, shards):
        gates[step] = lax.ppermute(
            gates[step], "ctx", [(j, partner(j, step, shards)) for j in range(shards)]
        )
    direct = size == TILE and width == TILE and lines % CHUNK == 0 and each <= 2
    if direct:
        scratch = [
            pltpu.VMEM((each + 1, 3, size, width), BF16),
            pltpu.VMEM((each + 1, 3, size, width), BF16),
            pltpu.VMEM((2 * size, width), F32),
            pltpu.VMEM((2, size, width), F32),
            pltpu.VMEM((each, 2, 2, size, width), BF16),
        ]
    else:
        scratch = [
            pltpu.VMEM((2 * each + 1, 2 * size, 2 * width), BF16),
            pltpu.VMEM((2 * each + 1, 2 * size, 2 * width), BF16),
            pltpu.VMEM((each, 2, 2 * size, width), BF16),
        ]
    convolved = pl.pallas_call(
        direct_conv_kernel if direct else conv_kernel,
        out_shape=jax.ShapeDtypeStruct(block, F32),
        in_specs=[vmem] * (2 + len(tables)),
        scratch_shapes=scratch,
        compiler_params=pltpu.CompilerParams(vmem_limit_bytes=20 * 2**20),
    )(data, weights, *tables)
    mixed = pl.pallas_call(
        gate_kernel,
        out_shape=jax.ShapeDtypeStruct(block, BF16),
        compiler_params=pltpu.CompilerParams(vmem_limit_bytes=12 * 2**20),
    )(convolved, *gates)
    own = lax.all_to_all(mixed, "ctx", split_axis=0, concat_axis=0, tiled=True)
    result = kernel_call(
        unpack_kernel, jax.ShapeDtypeStruct((each * shards, length), BF16), [work]
    )(own)
    return result[:channels]


def solution(mesh):
    return jax.shard_map(
        local,
        mesh=mesh,
        in_specs=(P("chan", "ctx"), P("chan", "ctx"), P("chan", "ctx"), P("chan")),
        out_specs=P("chan", "ctx"),
        check_vma=False,
    )
```

```python
import functools
import math

import jax
import jax.numpy as jnp
import numpy as np
from jax import lax
from jax.experimental import pallas as pl
from jax.experimental.pallas import tpu as pltpu
from jax.sharding import PartitionSpec as P

BF16 = jnp.bfloat16
F32 = jnp.float32


def two_parts(table):
    high = table.astype(BF16)
    low = (table - high.astype(np.float64)).astype(BF16)
    return np.stack([high, low])


def tables_of(rows, cols):
    total = rows * cols
    row = np.arange(rows, dtype=np.float64)
    col = np.arange(cols, dtype=np.float64)
    head = 2.0 * np.pi * ((4 * row[:, None] + 1) * row[None, :] % (4 * rows)) / (4 * rows)
    turn = 2.0 * np.pi * ((4 * row[:, None] + 1) * col[None, :]) / (4 * total)
    tail = 2.0 * np.pi * (col[:, None] * col[None, :] % cols) / cols
    twist = two_parts(np.concatenate([np.cos(turn), np.sin(turn)], 0))
    first = two_parts(np.concatenate([np.cos(head), np.sin(head)], 0))
    middle = two_parts(np.concatenate([np.cos(tail), np.sin(tail)], 0))
    last = two_parts(np.concatenate([np.cos(head).T, np.sin(head).T], 0) / total)
    kept = (twist, first, middle, last)
    shape = np.max([table.shape for table in kept], 0)
    return np.stack([np.pad(table, [(0, n) for n in shape - table.shape]) for table in kept])


def matmul(left, right):
    return jnp.dot(left, right, preferred_element_type=F32)


def split(value):
    high = value.astype(BF16)
    return high, (value - high.astype(F32)).astype(BF16)


LANES = 128


def spread(source_ref, work_ref, lines, first=0, count=None):
    channels, length = source_ref.shape
    width = length // lines
    for line in range(first, lines if count is None else first + count):
        for part in range(width // LANES):
            start = line * width + part * LANES
            work_ref[part, pl.ds(line, channels, stride=lines), :] = source_ref[
                :, start : start + LANES
            ].astype(F32)


POWER = 16
LIFT = 2.0 ** (126.0 / POWER)


def squeeze(value):
    scale = jnp.maximum(jnp.max(jnp.abs(value), 0, keepdims=True), 1e-30).astype(BF16)
    lifted = value * (LIFT / scale.astype(F32))
    power = lifted * lifted
    for _ in range(3):
        power = power * power
    return jnp.where(value < 0.0, -power, power).astype(BF16), scale


def unsqueeze(coded, scale):
    coded = coded.astype(F32)
    size = jnp.exp(jnp.log(jnp.abs(coded)) * (1.0 / POWER)) * (scale.astype(F32) * (1.0 / LIFT))
    return jnp.where(coded == 0.0, 0.0, jnp.where(coded < 0.0, -size, size))


def pack_kernel(*refs):
    source_hbm, taps_hbm, skip_hbm, out_hbm, weight_ref = refs[:5]
    source_ref, taps_ref, skip_ref, work_ref, tail_ref, out_ref = refs[5:11]
    in_sems, out_sems, skip_sem = refs[11:]
    channels, length = source_hbm.shape
    shards, rows, lines, width = out_hbm.shape
    each = rows - 1
    chunks = out_sems.shape[0]
    count = lines // chunks
    reads = []
    for chunk in range(chunks):
        span = pl.ds(chunk * count * width, count * width)
        reads.append(
            pltpu.make_async_copy(
                source_hbm.at[:, span], source_ref.at[:, span], in_sems.at[chunk]
            )
        )
    reads.append(pltpu.make_async_copy(taps_hbm, taps_ref, in_sems.at[chunks]))
    skip_read = pltpu.make_async_copy(skip_hbm, skip_ref, skip_sem)
    for read in [*reads, skip_read]:
        read.start()
    writes = []
    for chunk in range(chunks):
        first = chunk * count
        reads[chunk].wait()
        spread(source_ref, work_ref, lines, first, count)
        if chunk == 0:
            reads[chunks].wait()
        spread(taps_ref, tail_ref, lines, first, count)
        for part in range(width // LANES):
            span = slice(part * LANES, (part + 1) * LANES)
            taps = tail_ref[part, first : first + count, :].astype(BF16)
            for shard in range(shards):
                for row in range(each):
                    start = (shard * each + row) * lines + first
                    out_ref[shard, row, first : first + count, span] = work_ref[
                        part, start : start + count, :
                    ].astype(BF16)
                out_ref[shard, each, first : first + count, span] = taps
        span = pl.ds(first, count)
        write = pltpu.make_async_copy(
            out_ref.at[:, :, span, :], out_hbm.at[:, :, span, :], out_sems.at[chunk]
        )
        write.start()
        writes.append(write)
    skip_read.wait()
    position = lax.axis_index("ctx")
    for row in range(each):
        weight_ref[row] = jnp.full(weight_ref.shape[1:], skip_ref[position * each + row], F32)
    for write in writes:
        write.wait()


def load_kernel(tables_hbm, tables_ref, sem):
    copy = pltpu.make_async_copy(tables_hbm, tables_ref, sem)
    copy.start()
    copy.wait()


def conv_kernel(
    data_ref, weight_ref, tables_ref, out_ref, high_ref, low_ref, col_ref
):
    shards, rows, lines, width = data_ref.shape
    each = rows - 1
    size = shards * lines
    twist_ref, first_ref, middle_ref, last_ref = (
        tables_ref.at[index, :, :tall, :wide]
        for index, (tall, wide) in enumerate(
            ((2 * size, width), (2 * size, size), (2 * width, width), (2 * size, size))
        )
    )
    twist = twist_ref[0].astype(F32) + twist_ref[1].astype(F32)
    cosine, sine = twist[:size], twist[size:]

    def mixed(row):
        return (
            matmul(high_ref[row], middle_ref[0])
            + matmul(low_ref[row], middle_ref[0])
            + matmul(high_ref[row], middle_ref[1])
        )

    def forward(row):
        data = data_ref[:, row].reshape(size, width)
        part = matmul(first_ref[0], data) + matmul(first_ref[1], data)
        real, imag = part[:size], part[size:]
        real, imag = real * cosine - imag * sine, real * sine + imag * cosine
        for ref, pair in zip((high_ref, low_ref), zip(split(real), split(imag))):
            ref[row, :size, :width] = pair[0]
            ref[row, :size, width:] = -pair[1]
            ref[row, size:, :width] = pair[1]
            ref[row, size:, width:] = pair[0]

    for row in range(rows):
        forward(each - row)
    other = mixed(each)
    other_real, other_imag = other[:size], other[size:]
    for row in range(each):
        part = mixed(row)
        real, imag = part[:size], part[size:]
        real, imag = real * other_real - imag * other_imag, real * other_imag + imag * other_real
        for ref, pair in zip((high_ref, low_ref), zip(split(real), split(imag))):
            ref[rows + row, :size, :width] = pair[0]
            ref[rows + row, :size, width:] = pair[1]
            ref[rows + row, size:, :width] = pair[1]
            ref[rows + row, size:, width:] = -pair[0]
    for row in range(each):
        part = mixed(rows + row)
        real, imag = part[:size], part[size:]
        real, imag = real * cosine + imag * sine, imag * cosine - real * sine
        for index, pair in enumerate(zip(split(real), split(imag))):
            col_ref[row, index, :size] = pair[0]
            col_ref[row, index, size:] = pair[1]
    for row in range(each):
        result = 0.0
        for part in range(2):
            span = slice(part * size, (part + 1) * size)
            result += (
                matmul(last_ref[0, span], col_ref[row, 0, span])
                + matmul(last_ref[0, span], col_ref[row, 1, span])
                + matmul(last_ref[1, span], col_ref[row, 0, span])
            )
        weight = weight_ref[row, :1, :1]
        out_ref[:, row] = result.reshape(shards, lines, width) + weight * data_ref[:, row].astype(F32)


TILE = 256
CHUNK = 32


def direct_conv_kernel(*refs):
    kinds = [pltpu.ACC(unit)((CHUNK, TILE), F32) for unit in range(2) for _ in range(3 * TILE // CHUNK)]
    pl.run_scoped(functools.partial(direct_conv_body, *refs), *kinds)


def direct_conv_body(
    data_ref,
    weight_ref,
    tables_ref,
    out_ref,
    high_ref,
    low_ref,
    turn_ref,
    spec_ref,
    col_ref,
    *accs,
):
    shards, rows, lines, width = data_ref.shape
    each = rows - 1
    count = TILE // CHUNK
    half = count // 2
    accs = [accs[: 3 * count], accs[3 * count :]]
    twist_ref, first_ref, middle_ref, last_ref = (tables_ref.at[index] for index in range(4))
    units = range(2)
    channels = [list(range(unit, each, 2)) for unit in units]

    def push(unit, value, slot):
        pltpu.matmul_push_rhs(value, slot, unit)

    def add(unit, index, value, slot=None):
        pltpu.matmul_acc_lhs(accs[unit][index], value, slot)

    def pop(unit, index):
        return pltpu.matmul_pop(accs[unit][index])

    def chunk_of(index):
        return slice(index * CHUNK, (index + 1) * CHUNK)

    def store(row, index, real, imag, signs):
        for ref, (one, two) in zip((high_ref, low_ref), zip(split(real), split(imag))):
            ref[row, 0, chunk_of(index)] = one
            ref[row, 1, chunk_of(index)] = two
            ref[row, 2, chunk_of(index)] = -two if signs else -one

    def products(unit, slots, row_parts):
        for step, (part, tile) in enumerate(((0, 0), (0, 1), (1, 0), (1, 1))):
            slot = step % 2
            push(unit, middle_ref[part, tile * TILE : (tile + 1) * TILE], slot)
            load = slot
            for acc, operands, row, index in row_parts:
                refs = (high_ref, low_ref) if part == 0 else (high_ref,)
                for ref in refs:
                    add(unit, acc, ref[row, operands[tile], chunk_of(index)], load)
                    load = None

    for unit in units:
        push(unit, data_ref[:, each].reshape(TILE, TILE), 0)
    for unit in units:
        for index in range(count):
            span = slice(unit * TILE + index * CHUNK, unit * TILE + (index + 1) * CHUNK)
            add(unit, 2 * count + index, first_ref[0, span], 0 if index == 0 else None)
            add(unit, 2 * count + index, first_ref[1, span])
    for unit in units:
        for channel in channels[unit]:
            push(unit, data_ref[:, channel].reshape(TILE, TILE), 1)
            for index in range(count):
                for imag in range(2):
                    start = imag * TILE + index * CHUNK
                    span = slice(start, start + CHUNK)
                    load = 1 if index + imag == 0 else None
                    add(unit, 2 * index + imag, first_ref[0, span], load)
                    add(unit, 2 * index + imag, first_ref[1, span])

    for index in range(2 * count):
        span = chunk_of(index)
        turn_ref[span] = twist_ref[0, span].astype(F32) + twist_ref[1, span].astype(F32)

    def turn_of(index):
        return turn_ref[chunk_of(index)], turn_ref[chunk_of(count + index)]

    def turned(real, imag, index):
        cosine, sine = turn_of(index)
        return real * cosine - imag * sine, real * sine + imag * cosine

    for index in range(count):
        real, imag = pop(0, 2 * count + index), pop(1, 2 * count + index)
        store(each, index, *turned(real, imag, index), True)
    for unit in units:
        operands = (0, 2) if unit == 0 else (1, 0)
        products(unit, 0, [(2 * count + index, operands, each, index) for index in range(count)])
    for index in range(count):
        for unit in units:
            for channel in channels[unit]:
                real, imag = pop(unit, 2 * index), pop(unit, 2 * index + 1)
                store(channel, index, *turned(real, imag, index), True)
    for part in range(2):
        for unit in units:
            for channel in channels[unit]:
                products(
                    unit,
                    0,
                    [
                        (2 * index + imag, (1, 0) if imag else (0, 2), channel, index)
                        for index in range(part * half, (part + 1) * half)
                        for imag in range(2)
                    ],
                )
        if part == 0:
            for index in range(count):
                for unit in units:
                    spec_ref[unit, chunk_of(index)] = pop(unit, 2 * count + index)
    for part in range(2):
        for index in range(part * half, (part + 1) * half):
            other_real, other_imag = spec_ref[0, chunk_of(index)], spec_ref[1, chunk_of(index)]
            for unit in units:
                for channel in channels[unit]:
                    real, imag = pop(unit, 2 * index), pop(unit, 2 * index + 1)
                    store(
                        channel,
                        index,
                        real * other_real - imag * other_imag,
                        real * other_imag + imag * other_real,
                        False,
                    )
        for unit in units:
            for channel in channels[unit]:
                products(
                    unit,
                    0,
                    [
                        (2 * index + imag, (1, 2) if imag else (0, 1), channel, index)
                        for index in range(part * half, (part + 1) * half)
                        for imag in range(2)
                    ],
                )
    for index in range(count):
        cosine, sine = turn_of(index)
        for unit in units:
            for channel in channels[unit]:
                real, imag = pop(unit, 2 * index), pop(unit, 2 * index + 1)
                real, imag = real * cosine + imag * sine, imag * cosine - real * sine
                for place, pair in enumerate((split(real), split(imag))):
                    for part in range(2):
                        col_ref[channel, part, place, chunk_of(index)] = pair[part]
    for unit in units:
        for channel in channels[unit]:
            for step, (place, part) in enumerate(((0, 0), (1, 0), (0, 1), (1, 1))):
                slot = step % 2
                push(unit, col_ref[channel, part, place], slot)
                load = slot
                for index in range(count):
                    span = slice(place * TILE + index * CHUNK, place * TILE + (index + 1) * CHUNK)
                    for table in range(2 if part == 0 else 1):
                        add(unit, index, last_ref[table, span], load)
                        load = None
    for index in range(count):
        scales = []
        for channel in range(each):
            weight = jnp.concatenate([weight_ref[channel, :1]] * (width // LANES), 1)
            value = pop(channel % 2, index) + weight * data_ref[index, channel].astype(F32)
            coded, scale = squeeze(value)
            out_ref[index, channel * lines : (channel + 1) * lines] = coded
            scales.append(jnp.broadcast_to(scale.astype(F32), (8 // each, width)))
        out_ref[index, each * lines :] = jnp.concatenate(scales, 0).astype(BF16)


def finish(source, gate_ref, out_ref, work_ref):
    channels, length = out_ref.shape
    parts, rows, lanes = work_ref.shape
    lines = length // (parts * lanes)
    shards, each = source.shape
    for shard in range(shards):
        for row in range(each):
            value = source(shard, row)
            start = (shard * each + row) * lines
            for part in range(parts):
                work_ref[part, start : start + lines, :] = value[:, part * lanes : (part + 1) * lanes]
    for line in range(lines):
        for part in range(parts):
            start = (line * parts + part) * lanes
            span = slice(start, start + lanes)
            value = work_ref[part, pl.ds(line, channels, stride=lines), :]
            out_ref[:, span] = (gate_ref[:, span].astype(F32) * value).astype(BF16)


def coded_finish_kernel(source_ref, gate_ref, out_ref, work_ref):
    shards, tall, width = source_ref.shape
    channels, length = out_ref.shape
    each = channels // shards
    lines = (tall - 8) // each

    def source(shard, row):
        at = each * lines + row * (8 // each)
        return unsqueeze(
            source_ref[shard, row * lines : (row + 1) * lines], source_ref[shard, at : at + 1]
        )

    source.shape = (shards, each)
    finish(source, gate_ref, out_ref, work_ref)


def plain_finish_kernel(source_ref, gate_ref, out_ref, work_ref):
    def source(shard, row):
        return source_ref[shard, row]

    source.shape = source_ref.shape[:2]
    finish(source, gate_ref, out_ref, work_ref)


def in_hbm(value):
    return pltpu.with_memory_space_constraint(value, pltpu.HBM)


def kernel_call(body, out_shape, scratch=(), limit=12):
    return pl.pallas_call(
        body,
        out_shape=out_shape,
        scratch_shapes=list(scratch),
        compiler_params=pltpu.CompilerParams(vmem_limit_bytes=limit * 2**20),
    )


def local(signal, filter_taps, gate_values, skip_weight):
    channels, length = signal.shape
    shards = lax.axis_size("ctx")
    total = shards * length
    width = 1 << ((total.bit_length() - 1) // 2)
    lines = length // width
    size = shards * lines
    each = -(-channels // shards)
    spare = each * shards - channels
    skip = skip_weight
    gate = gate_values
    padded = signal
    if spare:
        padded = jnp.pad(signal, ((0, spare), (0, 0)))
        gate = jnp.pad(gate, ((0, spare), (0, 0)))
        skip = jnp.pad(skip, (0, spare))
    work = pltpu.VMEM((width // LANES, each * shards * lines, LANES), F32)
    block = (shards, each, lines, width)
    hbm = pl.BlockSpec(memory_space=pltpu.HBM)
    vmem = pl.BlockSpec(memory_space=pltpu.VMEM)
    chunks = max(1, lines // 16)
    packed, weights = pl.pallas_call(
        pack_kernel,
        out_shape=[
            jax.ShapeDtypeStruct((shards, each + 1, lines, width), BF16),
            jax.ShapeDtypeStruct((each, 8, LANES), F32),
        ],
        in_specs=[hbm] * 3,
        out_specs=[hbm, vmem],
        scratch_shapes=[
            pltpu.VMEM((each * shards, length), BF16),
            pltpu.VMEM((1, length), BF16),
            pltpu.SMEM((each * shards,), F32),
            work,
            pltpu.VMEM((width // LANES, lines, LANES), F32),
            pltpu.VMEM((shards, each + 1, lines, width), BF16),
            pltpu.SemaphoreType.DMA((chunks + 1,)),
            pltpu.SemaphoreType.DMA((chunks,)),
            pltpu.SemaphoreType.DMA,
        ],
        compiler_params=pltpu.CompilerParams(vmem_limit_bytes=12 * 2**20),
    )(*(in_hbm(value) for value in (padded, filter_taps, skip)))
    with jax.named_scope("first_swap"):
        data = lax.all_to_all(packed, "ctx", split_axis=0, concat_axis=0, tiled=True)
    tables = jnp.asarray(tables_of(size, width))
    tables = pl.pallas_call(
        load_kernel,
        out_shape=jax.ShapeDtypeStruct(tables.shape, BF16),
        in_specs=[hbm],
        out_specs=vmem,
        scratch_shapes=[pltpu.SemaphoreType.DMA],
        compiler_params=pltpu.CompilerParams(vmem_limit_bytes=(8 if size <= TILE else 32) * 2**20),
    )(in_hbm(tables))
    direct = size == TILE and width == TILE and lines == CHUNK and each <= 2 and not spare
    sent = jax.ShapeDtypeStruct(block, F32)
    if direct:
        sent = jax.ShapeDtypeStruct((shards, each * lines + 8, width), BF16)
    if direct:
        scratch = [
            pltpu.VMEM((each + 1, 3, size, width), BF16),
            pltpu.VMEM((each + 1, 3, size, width), BF16),
            pltpu.VMEM((2 * size, width), F32),
            pltpu.VMEM((2, size, width), F32),
            pltpu.VMEM((each, 2, 2, size, width), BF16),
        ]
    else:
        scratch = [
            pltpu.VMEM((2 * each + 1, 2 * size, 2 * width), BF16),
            pltpu.VMEM((2 * each + 1, 2 * size, 2 * width), BF16),
            pltpu.VMEM((each, 2, 2 * size, width), BF16),
        ]
    convolved = pl.pallas_call(
        direct_conv_kernel if direct else conv_kernel,
        out_shape=sent,
        in_specs=[vmem] * 3,
        scratch_shapes=scratch,
        compiler_params=pltpu.CompilerParams(vmem_limit_bytes=20 * 2**20),
    )(data, weights, tables)
    own = lax.all_to_all(convolved, "ctx", split_axis=0, concat_axis=0, tiled=True)
    result = kernel_call(
        coded_finish_kernel if direct else plain_finish_kernel,
        jax.ShapeDtypeStruct((each * shards, length), BF16),
        [work],
    )(own, gate)
    return result[:channels]


def solution(mesh):
    return jax.shard_map(
        local,
        mesh=mesh,
        in_specs=(P("chan", "ctx"), P("chan", "ctx"), P("chan", "ctx"), P("chan")),
        out_specs=P("chan", "ctx"),
        check_vma=False,
    )
```
